512 devices in a mesh: dp: 8 (over y), expert: 64 (over x, z, core).
Axes of the slice: x: 4, y: 8, z: 8, core: 2. Of those that a mesh axis runs over, the one named last changes fastest.
Arguments:
- tokens: bfloat16 [8192, 4096], P('expert', 'dp'), may hold values from -6 to 6
- cotangent: bfloat16 [8192, 4096], P('expert', 'dp'), may hold values from -6 to 6
- expert_ids: int32 [8192, 6], P('expert'), may hold values from 0 to 63, all different within a row; in each aligned block of 128 rows (0 to 127, 128 to 255, ...) at most 14 rows name the same one
- route_probs: bfloat16 [8192, 6], P('expert'), may hold values from 0.049804688 to 1
- w_gate: bfloat16 [64, 4096, 768], P('expert', 'dp'), may hold values from -0.09375 to 0.09375
- w_up: bfloat16 [64, 4096, 768], P('expert', 'dp'), may hold values from -0.09375 to 0.09375
- w_down: bfloat16 [64, 768, 4096], P('expert', None, 'dp'), may hold values from -0.09375 to 0.09375
Outputs:
- grad_tokens: bfloat16 [8192, 4096], P('expert', 'dp')
- grad_gate: bfloat16 [64, 4096, 768], P('expert', 'dp')
- grad_up: bfloat16 [64, 4096, 768], P('expert', 'dp')
- grad_down: bfloat16 [64, 768, 4096], P('expert', None, 'dp')
- d_probs: bfloat16 [8192, 6], P('expert')
The draws below stay inside these ranges and needn't reach their ends.
Inputs may be any that keep to these rules, and one draw needn't show every extreme that they name: `expert_ids`: each row names 6 different experts and every expert is named by some row; in each aligned block of 128 rows no expert is named by more than 14 rows, a bound that some block reaches.
All inputs are finite; a program needn't handle non-finite values.
Results may differ from the reference program's by a relative error of at most 0.024.
Values may be sent and summed in bfloat16 or wider, within the bound.
A program may use at most 64 MiB of HBM per device.

```python
import math
import jax
import jax.numpy as jnp
import numpy as np
from jax import lax

D = 4096
F = 768
TOP = 6
TOK = 128
EXPERTS = 64
TOKENS = 8192
CAP = 14
N_DP = 8
N_EXPERT = 64


def levels(stream_key, extent, split, smallest, top_value):
    factor_of = 1.0
    for dim, shards_of in split:
        draws = jax.random.uniform(jax.random.fold_in(jax.random.fold_in(stream_key, 6), dim), (shards_of,), jnp.float32, smallest / len(split), top_value / len(split))
        factor_of = factor_of * jnp.repeat(jnp.exp(draws), extent[dim] // shards_of).reshape((-1,) + (1,) * (len(extent) - 1 - dim))
    return factor_of


def deal_out(rng, own, number, rows, count, top, limit, lean):
    sequence = jax.random.permutation(rng, count)
    packed, ordinary = load_shares(count, rows * top, limit, lean, True), load_shares(count, rows * top, limit, lean, False)
    places = jnp.arange(count)

    def named(tallies, turn):
        used = int((tallies > 0).sum())
        fixed = max(1, used // 4)
        moved = fixed + (places - fixed + turn * (used - fixed)) % max(1, count - fixed)
        return jnp.zeros((count,), jnp.int32).at[sequence[jnp.where(places < fixed, places, moved)]].set(jnp.asarray(tallies, jnp.int32))

    tallies = jnp.where(number % 4 == 0, named(packed, number // 4), named(ordinary, number - number // 4 - 1))
    mixed = jax.random.permutation(jax.random.fold_in(own, 3), count)
    source_of, taker = mixed[0:count // 2 * 2:2], mixed[1:count // 2 * 2:2]
    slack = jnp.minimum(tallies[source_of] - 1, limit - tallies[taker]) // 2
    slack = jnp.where((source_of == sequence[0]) | (taker == sequence[0]) | (tallies[taker] == 0), 0, jnp.maximum(slack, 0))
    moved = jax.random.randint(jax.random.fold_in(own, 4), (count // 2,), 0, 1 << 20) % (slack + 1)
    tallies = tallies.at[source_of].add(-moved).at[taker].add(moved)
    members = jnp.searchsorted(jnp.cumsum(tallies), jnp.arange(rows * top), side="right").astype(jnp.int32)
    listing = members.reshape(top, rows).T
    listing = listing[jax.random.permutation(jax.random.fold_in(own, 1), rows)]
    turn = jax.random.randint(jax.random.fold_in(own, 2), (rows, 1), 0, top)
    return jnp.take_along_axis(listing, (jnp.arange(top)[None, :] + turn) % top, axis=1)


def load_shares(number_of, total, limit, lean, full):
    loads = [(1 << 20) // math.isqrt(standing ** lean) + 1 for standing in range(1, number_of + 1)]
    largest = limit if full else min(limit, max(-(-total // number_of), total * loads[0] // sum(loads)))
    least = 1 if total - largest >= number_of - 1 else 0
    counts, spare = [largest] + [least] * (number_of - 1), total - largest - least * (number_of - 1)
    while spare > 0:
        candidates = [i for i in range(1, number_of) if counts[i] < largest] or [i for i in range(1, number_of) if counts[i] < limit]
        whole, remaining = sum([loads[i] for i in candidates]), spare
        for i in candidates:
            addition = min(limit - counts[i], max(1, remaining * loads[i] // whole), spare)
            counts[i] = counts[i] + addition
            spare = spare - addition
    return np.array(counts)


def normal_values(key, shape, deviation, most, cuts=(), kind=jnp.bfloat16):
    drawn = jax.random.normal(key, shape, jnp.float32) * deviation
    if len(cuts) > 0:
        drawn = levels(key, shape, cuts, -0.22, 0.18) * drawn
    return jnp.clip(drawn, min=-most, max=most).astype(kind)


def setup_inputs(seed: int = 0) -> dict:
    streams_of = jax.random.split(jax.random.key(seed), 8)
    tokens = normal_values(streams_of[0], (TOKENS, D), 1.0, 6.0, ((0, 64), (1, 8)))
    cotangent = normal_values(streams_of[1], (TOKENS, D), 1.0, 6.0, ((0, 64), (1, 8)))
    expert_ids_keys = jax.random.split(jax.random.fold_in(streams_of[2], 1), TOKENS // TOK)
    expert_ids_turns = jax.random.permutation(jax.random.fold_in(streams_of[2], 3), TOKENS // TOK)
    expert_ids = jax.vmap(lambda own, number: deal_out(jax.random.fold_in(streams_of[2], 2), own, number, TOK, EXPERTS, TOP, CAP, 1))(expert_ids_keys, expert_ids_turns).reshape((TOKENS, TOP))
    route_probs = jnp.clip(jnp.exp(math.log(1.0) - 2.9996462 * jax.random.uniform(streams_of[3], (TOKENS, TOP), jnp.float32) ** levels(streams_of[3], (TOKENS, TOP), ((0, 64),), -0.2, 0.2)), 0.049804688, 1.0).astype(jnp.bfloat16)
    w_gate = normal_values(streams_of[4], (EXPERTS, D, F), D ** -0.5, 0.09375, ((0, 64), (1, 8)))
    w_up = normal_values(streams_of[5], (EXPERTS, D, F), D ** -0.5, 0.09375, ((0, 64), (1, 8)))
    w_down = normal_values(streams_of[6], (EXPERTS, F, D), D ** -0.5, 0.09375, ((0, 64), (2, 8)))
    return {"tokens": tokens, "cotangent": cotangent, "expert_ids": expert_ids, "route_probs": route_probs, "w_gate": w_gate, "w_up": w_up, "w_down": w_down}


def silu_parts(gate_sum):
    logistic = jax.nn.sigmoid(gate_sum)
    return gate_sum * logistic, logistic * (1.0 + gate_sum * (1.0 - logistic))


def rounded(partial_value):
    return lax.optimization_barrier(partial_value.astype(jnp.bfloat16)).astype(jnp.float32)


def reference(tokens, cotangent, expert_ids, route_probs, w_gate, w_up, w_down):
    block_cols = D // N_DP
    assigned = TOKENS * TOP
    rows_all = N_EXPERT * CAP
    flat_ids = expert_ids.reshape(N_EXPERT, TOK * TOP)
    onehot = (flat_ids[:, :, None] == jnp.arange(EXPERTS, dtype=jnp.int32)[None, None, :]).astype(jnp.int32)
    earlier = jnp.cumsum(onehot, axis=1) - onehot
    slot_index = jnp.sum(earlier * onehot, axis=2)
    anchor = jnp.arange(N_EXPERT, dtype=jnp.int32)[:, None]
    target = (flat_ids * rows_all + anchor * CAP + slot_index).reshape(-1).astype(jnp.int32)
    slot_table = jnp.full((EXPERTS * rows_all,), assigned, jnp.int32)
    slot_table = slot_table.at[target].set(jnp.arange(assigned, dtype=jnp.int32)).reshape(EXPERTS, rows_all)
    zero_row = jnp.zeros((1, D), jnp.bfloat16)
    x_pad = jnp.concatenate([tokens, zero_row], axis=0)
    dy_pad = jnp.concatenate([cotangent, zero_row], axis=0)
    p_pad = jnp.concatenate([route_probs.reshape(-1), jnp.zeros((1,), jnp.bfloat16)]).astype(jnp.float32)

    def one_expert(state_now, inputs):
        dx_acc, prob_acc = state_now
        row_ids, gate_w, up_w, down_w = inputs
        token_ids = row_ids // TOP
        x_rows = x_pad[token_ids]
        dy_rows = dy_pad[token_ids]
        p_rows = p_pad[row_ids]
        x_blocks = x_rows.astype(jnp.float32).reshape(rows_all, N_DP, block_cols)
        dy_blocks = dy_rows.astype(jnp.float32).reshape(rows_all, N_DP, block_cols)
        gate_blocks = gate_w.astype(jnp.float32).reshape(N_DP, block_cols, F)
        up_blocks = up_w.astype(jnp.float32).reshape(N_DP, block_cols, F)
        down_blocks = down_w.astype(jnp.float32).reshape(F, N_DP, block_cols)
        gate_sum = jnp.sum(rounded(jnp.einsum("rbd,bdf->brf", x_blocks, gate_blocks)), axis=0)
        up_sum = jnp.sum(rounded(jnp.einsum("rbd,bdf->brf", x_blocks, up_blocks)), axis=0)
        grad_h = jnp.sum(rounded(jnp.einsum("rbd,fbd->brf", dy_blocks, down_blocks)), axis=0)
        activated, derivative = silu_parts(gate_sum)
        hidden_f = rounded(activated * up_sum)
        prob_grad = jnp.sum(hidden_f * grad_h, axis=1)
        scaled = p_rows[:, None] * grad_h
        d_gate = (scaled * up_sum * derivative).astype(jnp.bfloat16)
        d_up = (scaled * activated).astype(jnp.bfloat16)
        h_scaled = (p_rows[:, None] * hidden_f).astype(jnp.bfloat16)
        dx_rows = (jnp.dot(d_gate, gate_w.T, preferred_element_type=jnp.float32)
                   + jnp.dot(d_up, up_w.T, preferred_element_type=jnp.float32)).astype(jnp.bfloat16)
        grad_g = jnp.dot(x_rows.T, d_gate, preferred_element_type=jnp.float32).astype(jnp.bfloat16)
        grad_u = jnp.dot(x_rows.T, d_up, preferred_element_type=jnp.float32).astype(jnp.bfloat16)
        grad_d = jnp.dot(h_scaled.T, dy_rows, preferred_element_type=jnp.float32).astype(jnp.bfloat16)
        dx_acc = dx_acc.at[token_ids].add(dx_rows.astype(jnp.float32))
        prob_acc = prob_acc.at[row_ids].add(prob_grad)
        return (dx_acc, prob_acc), (grad_g, grad_u, grad_d)

    start_state = (jnp.zeros((TOKENS + 1, D), jnp.float32), jnp.zeros((assigned + 1,), jnp.float32))
    final_state, grads_all = lax.scan(one_expert, start_state, (slot_table, w_gate, w_up, w_down))
    dx_acc, prob_acc = final_state
    grad_tokens = dx_acc[:TOKENS].astype(jnp.bfloat16)
    d_probs = prob_acc[:assigned].astype(jnp.bfloat16).reshape(TOKENS, TOP)
    return (grad_tokens, grads_all[0], grads_all[1], grads_all[2], d_probs)
```

```python
import jax
import jax.numpy as jnp
from jax import lax
from jax.sharding import PartitionSpec as P


def silu_parts(gate_sum):
    logistic = jax.nn.sigmoid(gate_sum)
    return (gate_sum * logistic, logistic * (1.0 + gate_sum * (1.0 - logistic)))


def local_step(gate_sum, up_sum, grad_h, gate_probs):
    activated, derivative = silu_parts(gate_sum)
    hidden_f = lax.optimization_barrier((activated * up_sum).astype(jnp.bfloat16)).astype(
        jnp.float32
    )
    prob_grad = jnp.sum(hidden_f * grad_h, axis=1).astype(jnp.bfloat16)
    scaled = gate_probs[:, None] * grad_h
    d_gate = (scaled * up_sum * derivative).astype(jnp.bfloat16)
    d_up = (scaled * activated).astype(jnp.bfloat16)
    h_scaled = (gate_probs[:, None] * hidden_f).astype(jnp.bfloat16)
    return (h_scaled, d_gate, d_up, prob_grad)


def contract_rows(a, b):
    return lax.dot_general(a, b, (((0,), (0,)), ((), ())), preferred_element_type=jnp.float32)


def contract_columns(a, b):
    return lax.dot_general(a, b, (((1,), (1,)), ((), ())), preferred_element_type=jnp.float32)


def exchange(rows):
    return lax.all_to_all(rows, "expert", split_axis=0, concat_axis=0, tiled=True)


def local(tokens, cotangent, expert_ids, route_probs, w_gate, w_up, w_down):
    expert_count = lax.axis_size("expert")
    token_count, columns = tokens.shape
    fanout = expert_ids.shape[1]
    capacity = max(2, 7 * token_count * fanout // (6 * expert_count))
    gate_w, up_w, down_w = w_gate[0], w_up[0], w_down[0]

    experts = jnp.arange(expert_count, dtype=jnp.int32)
    hits = expert_ids.T[:, None, :] == experts[None, :, None]
    chosen = jnp.any(hits, axis=0)
    order = jnp.arange(token_count, dtype=jnp.int32)
    before = (order[:, None] < order[None, :]).astype(jnp.bfloat16)
    earlier = jnp.dot(chosen.astype(jnp.bfloat16), before, preferred_element_type=jnp.float32)
    slot_of = jnp.where(chosen, earlier.astype(jnp.int32), -1)
    probs_f = route_probs.astype(jnp.float32)
    prob_of = jnp.sum(jnp.where(hits, probs_f.T[:, None, :], 0.0), axis=0)
    both = jnp.concatenate([tokens, cotangent], axis=1)

    chunks = ((0, 8), (8, capacity))
    ROWS = 8
    picks, received = [], []
    for first, last in chunks:
        slots = first + jnp.arange(ROWS, dtype=jnp.int32)
        wanted = jnp.where(slots < last, slots, -2)
        pick = (slot_of[:, None, :] == wanted[None, :, None]).astype(jnp.bfloat16)
        picks.append(pick.reshape(expert_count * ROWS, token_count))
    all_slots = jnp.arange(capacity, dtype=jnp.int32)
    sent_p = jnp.sum(
        jnp.where(slot_of[:, None, :] == all_slots[None, :, None], prob_of[:, None, :], 0.0), axis=2
    ).astype(jnp.bfloat16)
    p_row = jnp.pad(sent_p, ((0, 0), (0, 2 * columns - capacity)))
    for index, (first, last) in enumerate(chunks):
        rows = jnp.dot(picks[index], both, preferred_element_type=jnp.float32)
        rows = rows.astype(jnp.bfloat16).reshape(expert_count, ROWS, 2 * columns)
        if index == 1:
            row_id = jnp.arange(ROWS, dtype=jnp.int32)
            rows = jnp.where((row_id == ROWS - 1)[None, :, None], p_row[:, None, :], rows)
        if index == 1:
            rows, received[0] = lax.optimization_barrier((rows, received[0]))
        received.append(exchange(rows))
    recv_p = received[1][:, ROWS - 1, :capacity]

    parts = []
    for index, (first, last) in enumerate(chunks):
        got = received[index][:, : last - first].reshape(expert_count * (last - first), 2 * columns)
        x_rows, dy_rows = got[:, :columns], got[:, columns:]
        gate_part = jnp.dot(x_rows, gate_w, preferred_element_type=jnp.float32)
        up_part = jnp.dot(x_rows, up_w, preferred_element_type=jnp.float32)
        cot_part = contract_columns(dy_rows, down_w)
        sums = tuple(v.astype(jnp.bfloat16) for v in (gate_part, up_part, cot_part))
        parts.append((x_rows, dy_rows, sums))

    grads, backs, summed = [], [], None
    for index, (first, last) in enumerate(chunks):
        x_rows, dy_rows, sums = parts[index]
        if summed is not None:
            sums, summed = lax.optimization_barrier((sums, summed))
        reduced = tuple(lax.psum(v, "dp") for v in sums)
        summed = reduced
        parts[index] = (x_rows, dy_rows, reduced)
        if index == 1:
            pass
    for index, (first, last) in enumerate(chunks):
        x_rows, dy_rows, reduced = parts[index]
        count = last - first
        probs = recv_p[:, first:last].reshape(expert_count * count).astype(jnp.float32)
        gate_sum, up_sum, grad_h = (v.astype(jnp.float32) for v in reduced)
        h_scaled, d_gate, d_up, prob_grad = local_step(gate_sum, up_sum, grad_h, probs)
        dx_rows = contract_columns(d_gate, gate_w) + contract_columns(d_up, up_w)
        dx_rows = dx_rows.astype(jnp.bfloat16).reshape(expert_count, count, columns)
        prob_row = jnp.pad(prob_grad.reshape(expert_count, count), ((0, 0), (0, columns - count)))
        backs.append(exchange(jnp.concatenate([dx_rows, prob_row[:, None, :]], axis=1)))
        grads.append((contract_rows(x_rows, d_gate), contract_rows(x_rows, d_up),
                      contract_rows(h_scaled, dy_rows)))

    grad_gate, grad_up, grad_down = (a + b for a, b in zip(*grads))
    total = jnp.zeros((token_count, columns), jnp.float32)
    back_p = []
    for index, (first, last) in enumerate(chunks):
        count = last - first
        pick = picks[index].reshape(expert_count, ROWS, token_count)[:, :count]
        total += contract_rows(
            pick.reshape(expert_count * count, token_count),
            backs[index][:, :count].reshape(expert_count * count, columns),
        )
        back_p.append(backs[index][:, count, :count])
    back_p = jnp.concatenate(back_p, axis=1).astype(jnp.float32)
    back_of = jnp.sum(
        jnp.where(slot_of[:, None, :] == all_slots[None, :, None], back_p[:, :, None], 0.0), axis=1
    )
    d_probs = jnp.sum(jnp.where(hits, back_of[None], 0.0), axis=1).T.astype(jnp.bfloat16)
    return (
        total.astype(jnp.bfloat16),
        grad_gate.astype(jnp.bfloat16)[None],
        grad_up.astype(jnp.bfloat16)[None],
        grad_down.astype(jnp.bfloat16)[None],
        d_probs,
    )


def solution(mesh):
    in_specs = (
        P("expert", "dp"),
        P("expert", "dp"),
        P("expert", None),
        P("expert", None),
        P("expert", "dp", None),
        P("expert", "dp", None),
        P("expert", None, "dp"),
    )
    out_specs = (
        P("expert", "dp"),
        P("expert", "dp", None),
        P("expert", "dp", None),
        P("expert", None, "dp"),
        P("expert", None),
    )
    return jax.shard_map(local, mesh=mesh, in_specs=in_specs, out_specs=out_specs, check_vma=False)
```

```python
import jax
import jax.numpy as jnp
from jax import lax
from jax.sharding import PartitionSpec as P


def silu_parts(gate_sum):
    logistic = jax.nn.sigmoid(gate_sum)
    return (gate_sum * logistic, logistic * (1.0 + gate_sum * (1.0 - logistic)))


def local_step(gate_sum, up_sum, grad_h, gate_probs):
    activated, derivative = silu_parts(gate_sum)
    hidden_f = lax.optimization_barrier((activated * up_sum).astype(jnp.bfloat16)).astype(
        jnp.float32
    )
    prob_grad = jnp.sum(hidden_f * grad_h, axis=1).astype(jnp.bfloat16)
    scaled = gate_probs[:, None] * grad_h
    d_gate = (scaled * up_sum * derivative).astype(jnp.bfloat16)
    d_up = (scaled * activated).astype(jnp.bfloat16)
    h_scaled = (gate_probs[:, None] * hidden_f).astype(jnp.bfloat16)
    return (h_scaled, d_gate, d_up, prob_grad)


def contract_rows(a, b):
    return lax.dot_general(a, b, (((0,), (0,)), ((), ())), preferred_element_type=jnp.float32)


def contract_columns(a, b):
    return lax.dot_general(a, b, (((1,), (1,)), ((), ())), preferred_element_type=jnp.float32)


def exchange(rows):
    return lax.all_to_all(rows, "expert", split_axis=0, concat_axis=0, tiled=True)


def local(tokens, cotangent, expert_ids, route_probs, w_gate, w_up, w_down):
    expert_count = lax.axis_size("expert")
    token_count, columns = tokens.shape
    fanout = expert_ids.shape[1]
    capacity = max(2, 7 * token_count * fanout // (6 * expert_count))
    gate_w, up_w, down_w = w_gate[0], w_up[0], w_down[0]

    experts = jnp.arange(expert_count, dtype=jnp.int32)
    hits = expert_ids.T[:, None, :] == experts[None, :, None]
    chosen = jnp.any(hits, axis=0)
    order = jnp.arange(token_count, dtype=jnp.int32)
    before = (order[:, None] < order[None, :]).astype(jnp.bfloat16)
    earlier = jnp.dot(chosen.astype(jnp.bfloat16), before, preferred_element_type=jnp.float32)
    slot_of = jnp.where(chosen, earlier.astype(jnp.int32), -1)
    probs_f = route_probs.astype(jnp.float32)
    prob_of = jnp.sum(jnp.where(hits, probs_f.T[:, None, :], 0.0), axis=0)
    both = jnp.concatenate([tokens, cotangent], axis=1)

    all_slots = jnp.arange(capacity, dtype=jnp.int32)
    match = slot_of[:, None, :] == all_slots[None, :, None]
    padded = jnp.arange(capacity + 2, dtype=jnp.int32)
    pick = (slot_of[:, None, :] == padded[None, :, None]).astype(jnp.bfloat16)
    rows = jnp.dot(
        pick.reshape(expert_count * (capacity + 2), token_count),
        both,
        preferred_element_type=jnp.float32,
    ).astype(jnp.bfloat16).reshape(expert_count, capacity + 2, 2 * columns)
    sent_p = jnp.sum(jnp.where(match, prob_of[:, None, :], 0.0), axis=2).astype(jnp.bfloat16)
    p_row = jnp.pad(sent_p, ((0, 0), (0, 2 * columns - capacity)))
    rows = jnp.where((padded == capacity)[None, :, None], p_row[:, None, :], rows)
    received = exchange(rows)
    rows_all = expert_count * capacity
    gate_probs = received[:, capacity, :capacity].reshape(rows_all).astype(jnp.float32)
    got = received[:, :capacity].reshape(rows_all, 2 * columns)
    x_rows, dy_rows = got[:, :columns], got[:, columns:]
    parts = (
        jnp.dot(x_rows, gate_w, preferred_element_type=jnp.float32),
        jnp.dot(x_rows, up_w, preferred_element_type=jnp.float32),
        contract_columns(dy_rows, down_w),
    )
    gate_sum, up_sum, grad_h = (
        lax.psum(v.astype(jnp.bfloat16), "dp").astype(jnp.float32) for v in parts
    )
    h_scaled, d_gate, d_up, prob_grad = local_step(gate_sum, up_sum, grad_h, gate_probs)
    dx_rows = contract_columns(d_gate, gate_w) + contract_columns(d_up, up_w)
    dx_rows = dx_rows.astype(jnp.bfloat16).reshape(expert_count, capacity, columns)
    prob_row = jnp.pad(
        prob_grad.reshape(expert_count, capacity), ((0, 0), (0, columns - capacity))
    )
    back = exchange(jnp.concatenate([dx_rows, prob_row[:, None, :]], axis=1))
    grad_gate = contract_rows(x_rows, d_gate)
    grad_up = contract_rows(x_rows, d_up)
    grad_down = contract_rows(h_scaled, dy_rows)
    total = contract_rows(
        match.astype(jnp.bfloat16).reshape(rows_all, token_count),
        back[:, :capacity].reshape(rows_all, columns),
    )
    back_p = back[:, capacity, :capacity].astype(jnp.float32)
    back_of = jnp.sum(jnp.where(match, back_p[:, :, None], 0.0), axis=1)
    d_probs = jnp.sum(jnp.where(hits, back_of[None], 0.0), axis=1).T.astype(jnp.bfloat16)
    return (
        total.astype(jnp.bfloat16),
        grad_gate.astype(jnp.bfloat16)[None],
        grad_up.astype(jnp.bfloat16)[None],
        grad_down.astype(jnp.bfloat16)[None],
        d_probs,
    )


def solution(mesh):
    in_specs = (
        P("expert", "dp"),
        P("expert", "dp"),
        P("expert", None),
        P("expert", None),
        P("expert", "dp", None),
        P("expert", "dp", None),
        P("expert", None, "dp"),
    )
    out_specs = (
        P("expert", "dp"),
        P("expert", "dp", None),
        P("expert", "dp", None),
        P("expert", None, "dp"),
        P("expert", None),
    )
    return jax.shard_map(local, mesh=mesh, in_specs=in_specs, out_specs=out_specs, check_vma=False)
```

```python
import jax
import jax.numpy as jnp
from jax import lax
from jax.sharding import PartitionSpec as P


def silu_parts(gate_sum):
    logistic = jax.nn.sigmoid(gate_sum)
    return (gate_sum * logistic, logistic * (1.0 + gate_sum * (1.0 - logistic)))


def local_step(gate_sum, up_sum, grad_h, gate_probs):
    activated, derivative = silu_parts(gate_sum)
    hidden_f = lax.optimization_barrier((activated * up_sum).astype(jnp.bfloat16)).astype(
        jnp.float32
    )
    prob_grad = jnp.sum(hidden_f * grad_h, axis=1).astype(jnp.bfloat16)
    scaled = gate_probs[:, None] * grad_h
    d_gate = (scaled * up_sum * derivative).astype(jnp.bfloat16)
    d_up = (scaled * activated).astype(jnp.bfloat16)
    h_scaled = (gate_probs[:, None] * hidden_f).astype(jnp.bfloat16)
    return (h_scaled, d_gate, d_up, prob_grad)


def contract_rows(a, b):
    return lax.dot_general(a, b, (((0,), (0,)), ((), ())), preferred_element_type=jnp.float32)


def contract_columns(a, b):
    return lax.dot_general(a, b, (((1,), (1,)), ((), ())), preferred_element_type=jnp.float32)


def exchange(rows):
    return lax.all_to_all(rows, "expert", split_axis=0, concat_axis=0, tiled=True)


def sum_by_exchange(part, others):
    count = lax.axis_size("dp")
    slices = part.reshape(count, part.shape[0] // count, part.shape[1])
    slices = lax.all_to_all(slices, "dp", split_axis=0, concat_axis=0, tiled=True)
    total = jnp.sum(slices.astype(jnp.float32), axis=0).astype(jnp.bfloat16)
    total, others = lax.optimization_barrier((total, others))
    copies = jnp.broadcast_to(total[None], slices.shape)
    return lax.all_to_all(copies, "dp", split_axis=0, concat_axis=0, tiled=True).reshape(part.shape), others


def local(tokens, cotangent, expert_ids, route_probs, w_gate, w_up, w_down):
    expert_count = lax.axis_size("expert")
    token_count, columns = tokens.shape
    fanout = expert_ids.shape[1]
    capacity = max(2, 7 * token_count * fanout // (6 * expert_count))
    gate_w, up_w, down_w = w_gate[0], w_up[0], w_down[0]

    experts = jnp.arange(expert_count, dtype=jnp.int32)
    hits = expert_ids.T[:, None, :] == experts[None, :, None]
    chosen = jnp.any(hits, axis=0)
    order = jnp.arange(token_count, dtype=jnp.int32)
    before = (order[:, None] < order[None, :]).astype(jnp.bfloat16)
    earlier = jnp.dot(chosen.astype(jnp.bfloat16), before, preferred_element_type=jnp.float32)
    slot_of = jnp.where(chosen, earlier.astype(jnp.int32), -1)
    probs_f = route_probs.astype(jnp.float32)
    prob_of = jnp.sum(jnp.where(hits, probs_f.T[:, None, :], 0.0), axis=0)

    all_slots = jnp.arange(capacity, dtype=jnp.int32)
    match = slot_of[:, None, :] == all_slots[None, :, None]
    padded = jnp.arange(capacity + 2, dtype=jnp.int32)
    pick = (slot_of[:, None, :] == padded[None, :, None]).astype(jnp.bfloat16)
    pick = pick.reshape(expert_count * (capacity + 2), token_count)

    def rows_of(source):
        rows = jnp.dot(pick, source, preferred_element_type=jnp.float32).astype(jnp.bfloat16)
        return rows.reshape(expert_count, capacity + 2, columns)

    sent_p = jnp.sum(jnp.where(match, prob_of[:, None, :], 0.0), axis=2).astype(jnp.bfloat16)
    p_row = jnp.pad(sent_p, ((0, 0), (0, columns - capacity)))
    x_first = exchange(rows_of(tokens))
    dy_sent = jnp.where(
        (padded == capacity)[None, :, None], p_row[:, None, :], rows_of(cotangent)
    )
    x_first, dy_sent = lax.optimization_barrier((x_first, dy_sent))
    received = exchange(dy_sent)
    rows_all = expert_count * capacity
    x_rows = x_first[:, :capacity].reshape(rows_all, columns)
    gate_part = jnp.dot(x_rows, gate_w, preferred_element_type=jnp.float32).astype(jnp.bfloat16)
    up_part = jnp.dot(x_rows, up_w, preferred_element_type=jnp.float32).astype(jnp.bfloat16)
    others = (lax.psum(gate_part, "dp"), lax.psum(up_part, "dp"))
    gate_probs = received[:, capacity, :capacity].reshape(rows_all).astype(jnp.float32)
    dy_rows = received[:, :capacity].reshape(rows_all, columns)
    cot_part = contract_columns(dy_rows, down_w).astype(jnp.bfloat16)
    grad_h, others = sum_by_exchange(cot_part, others)
    gate_sum, up_sum, grad_h = (v.astype(jnp.float32) for v in (*others, grad_h))
    h_scaled, d_gate, d_up, prob_grad = local_step(gate_sum, up_sum, grad_h, gate_probs)
    dx_rows = contract_columns(d_gate, gate_w) + contract_columns(d_up, up_w)
    dx_rows = dx_rows.astype(jnp.bfloat16).reshape(expert_count, capacity, columns)
    prob_row = jnp.pad(
        prob_grad.reshape(expert_count, capacity), ((0, 0), (0, columns - capacity))
    )
    back = exchange(jnp.concatenate([dx_rows, prob_row[:, None, :]], axis=1))
    grad_gate = contract_rows(x_rows, d_gate)
    grad_up = contract_rows(x_rows, d_up)
    grad_down = contract_rows(h_scaled, dy_rows)
    total = contract_rows(
        match.astype(jnp.bfloat16).reshape(rows_all, token_count),
        back[:, :capacity].reshape(rows_all, columns),
    )
    back_p = back[:, capacity, :capacity].astype(jnp.float32)
    back_of = jnp.sum(jnp.where(match, back_p[:, :, None], 0.0), axis=1)
    d_probs = jnp.sum(jnp.where(hits, back_of[None], 0.0), axis=1).T.astype(jnp.bfloat16)
    return (
        total.astype(jnp.bfloat16),
        grad_gate.astype(jnp.bfloat16)[None],
        grad_up.astype(jnp.bfloat16)[None],
        grad_down.astype(jnp.bfloat16)[None],
        d_probs,
    )


def solution(mesh):
    in_specs = (
        P("expert", "dp"),
        P("expert", "dp"),
        P("expert", None),
        P("expert", None),
        P("expert", "dp", None),
        P("expert", "dp", None),
        P("expert", None, "dp"),
    )
    out_specs = (
        P("expert", "dp"),
        P("expert", "dp", None),
        P("expert", "dp", None),
        P("expert", None, "dp"),
        P("expert", None),
    )
    return jax.shard_map(local, mesh=mesh, in_specs=in_specs, out_specs=out_specs, check_vma=False)
```
